32 devices in a mesh: clus: 8 (over z, x), pair: 4 (over y, core).
Axes of the slice: x: 2, y: 2, z: 4, core: 2. Of those that a mesh axis runs over, the one named last changes fastest.
Arguments:
- child_basis: float32 [64, 256, 256], P('clus'), as said below
- transfer: float32 [64, 256, 256], P('clus'), may hold values from -0.5 to 0.5
- child_parent: int32 [8, 8], P('clus'), may hold values from 0 to 1, never falling along the last dimension, each value on 1 to 6 neighbouring positions
- upper_weight: float32 [16, 256, 256], P('clus'), as said below
- child_pairs: int32 [384, 2], P(('clus', 'pair')), may hold values from -1 to 63, as said below
- child_blocks: float32 [384, 256, 256], P(('clus', 'pair')), may hold values from -0.15625 to 0.15625
- parent_pairs: int32 [256, 2], P(('clus', 'pair')), may hold values from -1 to 15, as said below
- parent_blocks: float32 [256, 256, 256], P(('clus', 'pair')), may hold values from -0.15625 to 0.15625
Outputs:
- child_weight: float32 [64, 256, 256], P('clus')
- parent_basis: float32 [16, 256, 256], P('clus')
The draws below stay inside these ranges and needn't reach their ends.
Inputs may be any that keep to these rules, and one draw needn't show every extreme that they name: `child_pairs`: each device's aligned block of 12 rows holds its valid pairs first and then rows of -1, -1; every block has one valid row or more and some block is full. In the block of flat device index d (clus index c = d // 4), box i lies among the 8 boxes of clus index c, box j among those of clus indices c to c + 3, and j differs from i. `parent_pairs`: as for child_pairs, with blocks of 8 rows and the 2 parent boxes of each clus index. `child_basis`: symmetric positive definite. `upper_weight`: symmetric positive definite.
All inputs are finite; a program needn't handle non-finite values.
Results may differ from the reference program's by a relative error of at most 0.0003.
Values sent between devices are 32-bit elements; how exact they have to be, the bound alone decides.
A program may use at most 128 MiB of HBM per device.

```python
import math
import jax
import jax.numpy as jnp
import numpy as np
from jax import lax

RANK = 256
CHILD_DEV = 8
CPAIR_DEV = 12
PPAIR_DEV = 8
REACH = 3
MOST_KIDS = 6
PARENT_DEV = 2
NCHILD = 64
NPARENT = 16
NCPAIR = 384
NPPAIR = 256
N_CLUS = 8
N_PAIR = 4


def gram_draw(seed_key, box_total):
    subkeys = jax.random.split(seed_key, 2)
    diagonal = jnp.exp(jax.random.uniform(subkeys[0], (box_total, RANK), jnp.float32, math.log(2.5), math.log(6.0)))
    symmetric = jax.random.normal(subkeys[1], (box_total, RANK, RANK), jnp.float32)
    symmetric = (symmetric + jnp.swapaxes(symmetric, 1, 2)) / math.sqrt(2.0 * RANK)
    gram_set = symmetric + diagonal[:, :, None] * jnp.eye(RANK, dtype=jnp.float32)[None]
    return gram_set.astype(jnp.float32)


def pair_draw(seed_key, per_device, box_count):
    device_total = N_CLUS * N_PAIR
    total_rows = device_total * per_device
    row_ids = jnp.arange(total_rows, dtype=jnp.int32)
    device_ids = row_ids // per_device
    owner_ids = device_ids // N_PAIR
    slot_ids = row_ids % per_device
    subkeys = jax.random.split(seed_key, 5)
    near_local = jax.random.randint(subkeys[0], (total_rows,), 0, box_count, dtype=jnp.int32)
    reach_step = jax.random.randint(subkeys[1], (total_rows,), 0, REACH + 1, dtype=jnp.int32)
    far_owner = jnp.minimum(owner_ids + reach_step, N_CLUS - 1)
    far_local = jax.random.randint(subkeys[2], (total_rows,), 0, box_count, dtype=jnp.int32)
    marked = row_ids == total_rows - per_device
    near_local = jnp.where(marked, 0, near_local)
    far_local = jnp.where(marked, box_count - 1, far_local)
    far_owner = jnp.where(marked, N_CLUS - 1, far_owner)
    collide = (far_owner == owner_ids) & (far_local == near_local)
    far_local = jnp.where(collide, (near_local + 1) % box_count, far_local)
    counts = jax.random.randint(subkeys[3], (device_total,), per_device // 2, per_device, dtype=jnp.int32)
    chosen_device = jax.random.randint(subkeys[4], (), 0, device_total, dtype=jnp.int32)
    counts = jnp.where(jnp.arange(device_total, dtype=jnp.int32) == chosen_device, per_device, counts)
    usable = slot_ids < counts[device_ids]
    near_box = jnp.where(usable, owner_ids * box_count + near_local, -1)
    far_box = jnp.where(usable, far_owner * box_count + far_local, -1)
    return jnp.stack([near_box, far_box], axis=1).astype(jnp.int32)


def draw_child_basis(key, part):
    return gram_draw(jax.random.fold_in(key, 11), NCHILD)


def draw_upper_weight(key, part):
    return gram_draw(jax.random.fold_in(key, 12), NPARENT)


def draw_child_pairs(key, part):
    return pair_draw(jax.random.fold_in(key, 13), CPAIR_DEV, CHILD_DEV)


def draw_parent_pairs(key, part):
    return pair_draw(jax.random.fold_in(key, 14), PPAIR_DEV, PARENT_DEV)


def steps_of(key, shape, pieces, smallest, largest):
    def one(dim, blocks):
        draws = jax.random.uniform(jax.random.fold_in(jax.random.fold_in(key, 6), dim), (blocks,), jnp.float32, smallest / len(pieces), largest / len(pieces))
        return jnp.repeat(jnp.exp(draws), shape[dim] // blocks).reshape((-1,) + (1,) * (len(shape) - dim - 1))

    gain = one(*pieces[0])
    for cut in pieces[1:]:
        gain = gain * one(*cut)
    return gain


def length_profile(number_of, total, reach, slope):
    weights = [(1 << 20) // math.isqrt(grade ** slope) + 1 for grade in range(2, number_of + 1)]
    rest, given = total - reach - (number_of - 1), [1] * (number_of - 1)
    while rest > 0:
        free = [i for i in range(number_of - 1) if given[i] < reach]
        whole, remaining = sum([weights[i] for i in free]), rest
        for i in free:
            more = min(reach - given[i], max(1, remaining * weights[i] // whole), rest)
            given[i] = given[i] + more
            rest = rest - more
    return np.array([reach] + given)


def uneven_parts(rng, amount, total, reach, skew):
    if amount == 2:
        one = jax.random.randint(rng, (), max(1, total - reach), min(reach, total - 1) + 1)
        return jnp.stack([one, total - one])
    sizes = jnp.asarray(length_profile(amount, total, reach, skew), jnp.int32)
    twos = (amount - 1) // 2
    donor, taker = sizes[1:1 + 2 * twos:2], sizes[2:2 + 2 * twos:2]
    slack = jnp.minimum(donor - 1, reach - taker)
    passed = jax.random.randint(jax.random.fold_in(rng, 1), (twos,), 0, 1 << 20) % (slack + 1)
    sizes = sizes.at[1:1 + 2 * twos:2].set(donor - passed).at[2:2 + 2 * twos:2].set(taker + passed)
    return sizes[jax.random.permutation(jax.random.fold_in(rng, 2), amount)]


def normal_values(own_key, shape, width, limit, shards=(), kind=jnp.bfloat16):
    values = jax.random.normal(own_key, shape, jnp.float32) * width
    if len(shards) > 0:
        values = steps_of(own_key, shape, shards, -0.22, 0.18) * values
    return jnp.clip(values, min=-limit, max=limit).astype(kind)


def setup_inputs(seed: int = 0) -> dict:
    arg_keys = jax.random.split(jax.random.key(seed), 9)
    child_basis = draw_child_basis(jax.random.fold_in(arg_keys[8], 71), 0)
    transfer = normal_values(arg_keys[1], (NCHILD, RANK, RANK), (0.5 / RANK ** 0.5), 0.5, ((0, 8),), jnp.float32)
    child_parent = jax.vmap(lambda own: jnp.searchsorted(jnp.cumsum(uneven_parts(own, PARENT_DEV, CHILD_DEV, MOST_KIDS, 1)), jnp.arange(CHILD_DEV), side="right"))(jax.random.split(arg_keys[2], N_CLUS)).reshape((N_CLUS, CHILD_DEV)).astype(jnp.int32)
    upper_weight = draw_upper_weight(jax.random.fold_in(arg_keys[8], 71), 0)
    child_pairs = draw_child_pairs(jax.random.fold_in(arg_keys[8], 71), 0)
    child_blocks = normal_values(arg_keys[5], (NCPAIR, RANK, RANK), (1.0 / (6 * RANK ** 0.5)), 0.15625, ((0, 32),), jnp.float32)
    parent_pairs = draw_parent_pairs(jax.random.fold_in(arg_keys[8], 71), 0)
    parent_blocks = normal_values(arg_keys[7], (NPPAIR, RANK, RANK), (1.0 / (6 * RANK ** 0.5)), 0.15625, ((0, 32),), jnp.float32)
    return dict(child_basis=child_basis, transfer=transfer, child_parent=child_parent, upper_weight=upper_weight, child_pairs=child_pairs, child_blocks=child_blocks, parent_pairs=parent_pairs, parent_blocks=parent_blocks)


HIGHEST = lax.Precision.HIGHEST


def coupling(pair_list, blocks, gram_set, per_block):
    extent = gram_set.shape[-1]
    box_total = gram_set.shape[0]
    grouped = pair_list.reshape(-1, per_block, 2)
    stacked = blocks.reshape(-1, per_block, extent, extent)

    def advance(weight, element):
        group_pairs, group_blocks = element
        usable = group_pairs[:, 0] >= 0
        near_index = jnp.where(usable, group_pairs[:, 0], 0).astype(jnp.int32)
        far_index = jnp.where(usable, group_pairs[:, 1], 0).astype(jnp.int32)
        near_gram = gram_set[near_index]
        far_gram = gram_set[far_index]
        near_term = jnp.einsum("pab,pbc->pac", group_blocks, far_gram, precision=HIGHEST)
        near_term = jnp.einsum("pac,pdc->pad", near_term, group_blocks, precision=HIGHEST)
        far_term = jnp.einsum("pba,pbc->pac", group_blocks, near_gram, precision=HIGHEST)
        far_term = jnp.einsum("pac,pcd->pad", far_term, group_blocks, precision=HIGHEST)
        factor = usable.astype(gram_set.dtype)[:, None, None]
        weight = weight.at[near_index].add(near_term * factor)
        weight = weight.at[far_index].add(far_term * factor)
        return weight, None

    start = jnp.zeros((box_total, extent, extent), gram_set.dtype)
    weight, unused = lax.scan(advance, start, (grouped, stacked))
    return weight


def reference(child_basis, transfer, child_parent, upper_weight, child_pairs, child_blocks, parent_pairs, parent_blocks):
    extent = child_basis.shape[-1]
    parent_index = ((jnp.arange(NCHILD) // CHILD_DEV) * PARENT_DEV + child_parent.reshape(-1)).astype(jnp.int32)
    lifted = jnp.einsum("cba,cbd->cad", transfer, child_basis, precision=HIGHEST)
    lifted = jnp.einsum("cad,cde->cae", lifted, transfer, precision=HIGHEST)
    parent_basis = jnp.zeros((NPARENT, extent, extent), child_basis.dtype).at[parent_index].add(lifted)
    parent_weight = upper_weight + coupling(parent_pairs, parent_blocks, parent_basis, PPAIR_DEV)
    chosen = parent_weight[parent_index]
    lowered = jnp.einsum("cab,cbd->cad", transfer, chosen, precision=HIGHEST)
    lowered = jnp.einsum("cad,ced->cae", lowered, transfer, precision=HIGHEST)
    child_weight = coupling(child_pairs, child_blocks, child_basis, CPAIR_DEV) + lowered
    return child_weight, parent_basis
```

```python
import functools

import jax
import jax.numpy as jnp
from jax import lax
from jax.experimental import pallas as pl
from jax.experimental.pallas import tpu as pltpu
from jax.sharding import PartitionSpec as P

REACH = 3
CORES = 2
MESH = pl.DeviceIdType.MESH
F32 = jnp.float32
VMEM = pl.BlockSpec(memory_space=pltpu.VMEM)
SMEM = pl.BlockSpec(memory_space=pltpu.SMEM)


def split(x):
    hi = x.astype(jnp.bfloat16)
    return hi, (x - hi.astype(F32)).astype(jnp.bfloat16)


def product(a, b, dims):
    (ah, al), (bh, bl) = a, b
    dot = functools.partial(
        lax.dot_general, dimension_numbers=(dims, ((), ())), preferred_element_type=F32
    )
    return dot(ah, bh) + (dot(ah, bl) + dot(al, bh))


NN = ((1,), (0,))
NT = ((1,), (1,))
TN = ((0,), (0,))


def pack(x):
    h, q = x.shape[0] // 2, x.shape[0] // 4
    low = jnp.concatenate([x[h : h + q, h:], x[h + q :, h:]], axis=1)
    return jnp.concatenate([x[:h], low], axis=0)


def unpack(p):
    n = p.shape[1]
    h, q = n // 2, n // 4
    top = p[:h]
    corner = jnp.concatenate([p[h:, :h], p[h:, h:]], axis=0)
    low = jnp.concatenate([top[:, h:].T, corner], axis=1)
    return jnp.concatenate([top, low], axis=0)


def loop(count, body):
    lax.fori_loop(0, count, lambda i, c: (body(i), c)[1], 0)


def outer_product(s, g):
    s, g = split(s), split(g)
    return product(split(product(s, g, NN)), s, NT)


def inner_product(s, g):
    s, g = split(s), split(g)
    return product(s, split(product(g, s, NN)), TN)


def far_kernel(
    boxes, parents,
    basis, transfer, child_parent, cpairs, cblocks, ppairs, pblocks,
    pbasis, basis_p, pbasis_p, far, pfar,
):
    clus = lax.axis_index("clus")
    pbasis[...] = jnp.zeros_like(pbasis)
    far[...] = jnp.zeros_like(far)
    pfar[...] = jnp.zeros_like(pfar)

    def lift(c):
        g = basis[c]
        basis_p[c] = pack(g)
        p = child_parent[0, c]
        pbasis[p] += inner_product(transfer[c], g)

    loop(boxes, lift)

    def terms(pairs, blocks, grams, sums, count):
        def one(r):
            i, j = pairs[r, 0], pairs[r, 1]

            @pl.when(i >= 0)
            def _():
                t = inner_product(blocks[r], grams[i - clus * count])
                sums[j - clus * count] += pack(t)

        loop(blocks.shape[0], one)

    for p in range(parents):
        pbasis_p[p] = pack(pbasis[p])
    terms(ppairs, pblocks, pbasis, pfar, parents)
    terms(cpairs, cblocks, basis, far, boxes)


def near_kernel(
    boxes, parents, scale,
    cpairs, cblocks, win, ppairs, pblocks, pwin, upper,
    near, pnear,
):
    clus = lax.axis_index("clus")
    near[...] = jnp.zeros_like(near)
    for p in range(parents):
        pnear[p] = pack(upper[p]) * scale

    def terms(pairs, blocks, grams, sums, count):
        def one(r):
            i, j = pairs[r, 0], pairs[r, 1]

            @pl.when(i >= 0)
            def _():
                t = outer_product(blocks[r], unpack(grams[j - clus * count]))
                sums[i - clus * count] += pack(t)

        loop(blocks.shape[0], one)

    terms(ppairs, pblocks, pwin, pnear, parents)
    terms(cpairs, cblocks, win, near, boxes)


def remote(src, dst, sems, index, device):
    send, recv = sems
    return pltpu.make_async_remote_copy(
        src_ref=src, dst_ref=dst, send_sem=send.at[index], recv_sem=recv.at[index],
        device_id=device, device_id_type=MESH,
    )


def place():
    clus, n = lax.axis_index("clus"), lax.axis_size("clus")
    pair = lax.axis_index("pair")
    rows = lax.axis_size("pair") // CORES
    return clus, n, pair // CORES, rows, pair % CORES


def at_pair(clus, y, k):
    return (clus, y * CORES + k)


def meet(clus, n, y, rows, k, along):
    barrier = pltpu.get_barrier_semaphore()

    def tell(device):
        pl.semaphore_signal(barrier, inc=1, device_id=device, device_id_type=MESH)

    tell(at_pair(clus, y, 1 - k))
    for d in range(1, rows):
        tell(at_pair(clus, (y + d) % rows, k))
    peers = rows
    if along:
        for o in range(1, REACH + 1):
            for ok, other in ((clus >= o, clus - o), (clus + o < n, clus + o)):
                @pl.when(ok)
                def _():
                    tell(at_pair(other, y, k))
                peers = peers + ok.astype(jnp.int32)
    pl.semaphore_wait(barrier, peers)


def exchange_kernel(
    boxes, parents,
    basis_p, pbasis_p, far, pfar,
    win, pwin, own, pown,
    half_in, phalf_in, half, phalf, row_in, mine, up_in, pup_in,
    down_s, down_r, pdown_s, pdown_r, core_s, core_r, pcore_s, pcore_r,
    row_s, row_r, up_s, up_r, pup_s, pup_r, fwd_s, fwd_r, pfwd_s, pfwd_r, local_sem,
):
    clus, n, y, rows, k = place()
    hb, ph = boxes // CORES, parents // CORES
    qb = hb // rows
    meet(clus, n, y, rows, k, True)
    partner = at_pair(clus, y, 1 - k)
    reach = range(1, REACH + 1)
    backward = range(REACH, -1, -1)
    keep, give = pl.ds(k * hb, hb), pl.ds((1 - k) * hb, hb)
    pkeep, pgive = pl.ds(k * ph, ph), pl.ds((1 - k) * ph, ph)
    local = pltpu.make_async_copy(basis_p, win.at[0], local_sem.at[0])
    plocal = pltpu.make_async_copy(pbasis_p, pwin.at[0], local_sem.at[1])
    local.start()
    plocal.start()

    core = [remote(far.at[o, give], half_in.at[o], (core_s, core_r), o, partner)
            for o in range(REACH + 1)]
    pcore = [remote(pfar.at[o, pgive], phalf_in.at[o], (pcore_s, pcore_r), o, partner)
             for o in range(REACH + 1)]
    down, pdown = {}, {}
    for o in reach:
        to = at_pair(clus - o, y, k)
        down[o] = remote(basis_p.at[keep], win.at[o, keep], (down_s, down_r), o, to)
        pdown[o] = remote(pbasis_p.at[pkeep], pwin.at[o, pkeep], (pdown_s, pdown_r), o, to)
    for o in backward:
        pcore[o].start()
        core[o].start()
    for o in reach:
        @pl.when(clus >= o)
        def _():
            pdown[o].start()
    for o in reach:
        @pl.when(clus >= o)
        def _():
            down[o].start()

    row = {}
    pup, up = {}, {}
    for o in backward:
        pcore[o].wait_recv()
        phalf[o] = pfar[o, pkeep] + phalf_in[o]
        if o:
            pup[o] = remote(phalf.at[o], pup_in.at[o - 1], (pup_s, pup_r), o, at_pair(clus + o, y, k))

            @pl.when(clus + o < n)
            def _():
                pup[o].start()
    for o in backward:
        core[o].wait_recv()
        half[o] = far[o, keep] + half_in[o]
        for d in range(1, rows):
            to = (y + d) % rows
            row[o, d] = remote(
                half.at[o, pl.ds(to * qb, qb)], row_in.at[o, d - 1], (row_s, row_r),
                o * (rows - 1) + d - 1, at_pair(clus, to, k),
            )
            row[o, d].start()
    for o in backward:
        total = half[o, pl.ds(y * qb, qb)]
        for d in range(1, rows):
            row[o, d].wait_recv()
            total = total + row_in[o, d - 1]
        mine[o] = total
        if o:
            up[o] = remote(mine.at[o], up_in.at[o - 1], (up_s, up_r), o, at_pair(clus + o, y, k))

            @pl.when(clus + o < n)
            def _():
                up[o].start()

    fwd, pfwd = {}, {}
    for o in reach:
        fwd[o] = remote(win.at[o, keep], win.at[o, keep], (fwd_s, fwd_r), o, partner)
        pfwd[o] = remote(pwin.at[o, pkeep], pwin.at[o, pkeep], (pfwd_s, pfwd_r), o, partner)
    for o in reach:
        @pl.when(clus + o < n)
        def _():
            pdown[o].wait_recv()
            pfwd[o].start()
    for o in reach:
        @pl.when(clus + o < n)
        def _():
            down[o].wait_recv()
            fwd[o].start()

    own[...] = mine[0]
    pown[...] = phalf[0]
    for o in reach:
        @pl.when(clus >= o)
        def _():
            pup[o].wait_recv()
            pown[...] += pup_in[o - 1]
            up[o].wait_recv()
            own[...] += up_in[o - 1]
    local.wait()
    plocal.wait()
    for o in reach:
        @pl.when(clus + o < n)
        def _():
            pfwd[o].wait()
            fwd[o].wait()
            up[o].wait_send()
            pup[o].wait_send()

        @pl.when(clus >= o)
        def _():
            down[o].wait_send()
            pdown[o].wait_send()
    for o in range(REACH + 1):
        core[o].wait_send()
        pcore[o].wait_send()
        for d in range(1, rows):
            row[o, d].wait_send()


def finish_kernel(
    boxes, parents,
    near, pnear, own, pown, transfer, child_parent,
    out,
    half_in, phalf_in, weight, pwork, total, row_in,
    core_s, core_r, pcore_s, pcore_r, pw_s, pw_r, row_s, row_r, gat_s, gat_r, fwd_s, fwd_r,
):
    clus, n, y, rows, k = place()
    hb, ph = boxes // CORES, parents // CORES
    qb = hb // rows
    meet(clus, n, y, rows, k, False)
    partner = at_pair(clus, y, 1 - k)
    pkeep, pgive = pl.ds(k * ph, ph), pl.ds((1 - k) * ph, ph)
    pcore = remote(pnear.at[pgive], phalf_in, (pcore_s, pcore_r), 0, partner)
    core = remote(near.at[pl.ds((1 - k) * hb, hb)], half_in, (core_s, core_r), 0, partner)
    pcore.start()
    core.start()
    pcore.wait_recv()
    pwork[...] = pnear[pkeep] + phalf_in[...] + pown[...]
    weight[pkeep] = pwork[...]
    pw = remote(pwork, weight.at[pkeep], (pw_s, pw_r), 0, partner)
    pw.start()
    core.wait_recv()
    total[...] = near[pl.ds(k * hb, hb)] + half_in[...]
    pw.wait_recv()

    def lower(b):
        c = k * hb + b
        w = unpack(weight[child_parent[0, c]])
        total[b] += pack(outer_product(transfer[c], w))

    row = []
    for d in list(range(1, rows)) + [0]:
        to = (y + d) % rows
        loop(qb, lambda q: lower(to * qb + q))
        if d:
            copy = remote(
                total.at[pl.ds(to * qb, qb)], row_in.at[d - 1], (row_s, row_r), d - 1,
                at_pair(clus, to, k),
            )
            copy.start()
            row.append(copy)
    result = total[pl.ds(y * qb, qb)] + own[...]
    for d in range(1, rows):
        row[d - 1].wait_recv()
        result = result + row_in[d - 1]
    here = pl.ds(k * hb + y * qb, qb)
    out[here] = result
    gather = [
        remote(out.at[here], out.at[here], (gat_s, gat_r), d - 1, at_pair(clus, (y + d) % rows, k))
        for d in range(1, rows)
    ]
    for copy in gather:
        copy.start()
    forward = []
    for d in range(rows):
        there = here
        if d:
            gather[d - 1].wait_recv()
            there = pl.ds(k * hb + (y + rows - d) % rows * qb, qb)
        copy = remote(out.at[there], out.at[there], (fwd_s, fwd_r), d, partner)
        copy.start()
        forward.append(copy)
    for copy in forward:
        copy.wait()
    for copy in gather + row + [core, pcore, pw]:
        copy.wait_send()


def unpack_kernel(packed, out):
    out[0] = unpack(packed[0])


def per_device(
    child_basis, transfer, child_parent, upper_weight, child_pairs, child_blocks,
    parent_pairs, parent_blocks,
):
    boxes, extent = child_basis.shape[0], child_basis.shape[-1]
    parents = upper_weight.shape[0]
    rows = lax.axis_size("pair") // CORES
    hb, ph = boxes // CORES, parents // CORES
    qb = hb // rows
    spans = REACH + 1
    tall = extent * 3 // 4
    shape = lambda *lead: jax.ShapeDtypeStruct(lead + (tall, extent), F32)
    room = lambda *lead: pltpu.VMEM(lead + (tall, extent), F32)
    sems = lambda *counts: [pltpu.SemaphoreType.DMA((c,)) for c in counts for _ in range(2)]

    pbasis, basis_p, pbasis_p, far, pfar = pl.pallas_call(
        functools.partial(far_kernel, boxes, parents),
        out_shape=(
            jax.ShapeDtypeStruct(upper_weight.shape, F32),
            shape(boxes), shape(parents), shape(spans * boxes), shape(spans * parents),
        ),
        in_specs=[VMEM, VMEM, SMEM, SMEM, VMEM, SMEM, VMEM],
        out_specs=(VMEM,) * 5,
        name="far_terms",
    )(child_basis, transfer, child_parent, child_pairs, child_blocks, parent_pairs, parent_blocks)

    win, pwin, own, pown = pl.pallas_call(
        functools.partial(exchange_kernel, boxes, parents),
        out_shape=(shape(spans, boxes), shape(spans, parents), shape(qb), shape(ph)),
        in_specs=[VMEM] * 4,
        out_specs=(VMEM,) * 4,
        scratch_shapes=[
            room(spans, hb), room(spans, ph), room(spans, hb), room(spans, ph),
            room(spans, max(rows - 1, 1), qb), room(spans, qb), room(REACH, qb), room(REACH, ph),
        ]
        + sems(spans, spans, spans, spans, spans * max(rows - 1, 1), spans, spans, spans, spans)
        + [pltpu.SemaphoreType.DMA((2,))],
        compiler_params=pltpu.CompilerParams(collective_id=0, has_side_effects=True),
        name="exchange",
    )(
        basis_p, pbasis_p,
        far.reshape(spans, boxes, tall, extent), pfar.reshape(spans, parents, tall, extent),
    )

    near, pnear = pl.pallas_call(
        functools.partial(near_kernel, boxes, parents, 1.0 / (rows * CORES)),
        out_shape=(shape(boxes), shape(parents)),
        in_specs=[SMEM, VMEM, VMEM, SMEM, VMEM, VMEM, VMEM],
        out_specs=(VMEM,) * 2,
        name="near_terms",
    )(
        child_pairs, child_blocks, win.reshape(spans * boxes, tall, extent),
        parent_pairs, parent_blocks, pwin.reshape(spans * parents, tall, extent), upper_weight,
    )

    packed = pl.pallas_call(
        functools.partial(finish_kernel, boxes, parents),
        out_shape=shape(boxes),
        in_specs=[VMEM] * 5 + [SMEM],
        out_specs=VMEM,
        scratch_shapes=[
            room(hb), room(ph), room(parents), room(ph), room(hb), room(max(rows - 1, 1), qb),
        ]
        + sems(1, 1, 1, max(rows - 1, 1), max(rows - 1, 1), rows),
        compiler_params=pltpu.CompilerParams(collective_id=1, has_side_effects=True),
        name="finish",
    )(near, pnear, own, pown, transfer, child_parent)

    child_weight = pl.pallas_call(
        unpack_kernel,
        grid=(boxes,),
        out_shape=jax.ShapeDtypeStruct(child_basis.shape, F32),
        in_specs=[pl.BlockSpec((1, tall, extent), lambda b: (b, 0, 0))],
        out_specs=pl.BlockSpec((1, extent, extent), lambda b: (b, 0, 0)),
        name="unfold",
    )(packed)
    return (child_weight, pbasis)


def solution(mesh):
    return jax.shard_map(
        per_device,
        mesh=mesh,
        in_specs=(
            P("clus", None, None),
            P("clus", None, None),
            P("clus", None),
            P("clus", None, None),
            P(("clus", "pair"), None),
            P(("clus", "pair"), None, None),
            P(("clus", "pair"), None),
            P(("clus", "pair"), None, None),
        ),
        out_specs=(P("clus", None, None), P("clus", None, None)),
        check_vma=False,
    )
```

```python
import functools

import jax
import jax.numpy as jnp
from jax import lax
from jax.experimental import pallas as pl
from jax.experimental.pallas import tpu as pltpu
from jax.sharding import PartitionSpec as P

REACH = 3
CORES = 2
MESH = pl.DeviceIdType.MESH
F32 = jnp.float32
VMEM = pl.BlockSpec(memory_space=pltpu.VMEM)
SMEM = pl.BlockSpec(memory_space=pltpu.SMEM)


def split(x):
    hi = x.astype(jnp.bfloat16)
    return hi, (x - hi.astype(F32)).astype(jnp.bfloat16)


def product(a, b, dims):
    (ah, al), (bh, bl) = a, b
    dot = functools.partial(
        lax.dot_general, dimension_numbers=(dims, ((), ())), preferred_element_type=F32
    )
    return dot(ah, bh) + (dot(ah, bl) + dot(al, bh))


NN = ((1,), (0,))
NT = ((1,), (1,))
TN = ((0,), (0,))


def pack(x):
    h, q = x.shape[0] // 2, x.shape[0] // 4
    low = jnp.concatenate([x[h : h + q, h:], x[h + q :, h:]], axis=1)
    return jnp.concatenate([x[:h], low], axis=0)


def unpack(p):
    n = p.shape[1]
    h, q = n // 2, n // 4
    top = p[:h]
    corner = jnp.concatenate([p[h:, :h], p[h:, h:]], axis=0)
    low = jnp.concatenate([top[:, h:].T, corner], axis=1)
    return jnp.concatenate([top, low], axis=0)


def loop(count, body):
    lax.fori_loop(0, count, lambda i, c: (body(i), c)[1], 0)


def outer_product(s, g):
    s, g = split(s), split(g)
    return product(split(product(s, g, NN)), s, NT)


def inner_product(s, g):
    s, g = split(s), split(g)
    return product(s, split(product(g, s, NN)), TN)


def far_kernel(
    boxes, parents,
    basis, transfer, child_parent, cpairs, cblocks, ppairs, pblocks,
    pbasis, basis_p, pbasis_p, far, pfar,
):
    clus = lax.axis_index("clus")
    pbasis[...] = jnp.zeros_like(pbasis)
    far[...] = jnp.zeros_like(far)
    pfar[...] = jnp.zeros_like(pfar)

    def lift(c):
        g = basis[c]
        basis_p[c] = pack(g)
        p = child_parent[0, c]
        pbasis[p] += inner_product(transfer[c], g)

    loop(boxes, lift)

    def terms(pairs, blocks, grams, sums, count):
        def one(r):
            i, j = pairs[r, 0], pairs[r, 1]

            @pl.when(i >= 0)
            def _():
                t = inner_product(blocks[r], grams[i - clus * count])
                sums[j - clus * count] += pack(t)

        loop(blocks.shape[0], one)

    for p in range(parents):
        pbasis_p[p] = pack(pbasis[p])
    terms(ppairs, pblocks, pbasis, pfar, parents)
    terms(cpairs, cblocks, basis, far, boxes)


def near_kernel(
    boxes, parents, scale,
    cpairs, cblocks, win, ppairs, pblocks, pwin, upper,
    near, pnear,
):
    clus = lax.axis_index("clus")
    near[...] = jnp.zeros_like(near)
    for p in range(parents):
        pnear[p] = pack(upper[p]) * scale

    def terms(pairs, blocks, grams, sums, count):
        def one(r):
            i, j = pairs[r, 0], pairs[r, 1]

            @pl.when(i >= 0)
            def _():
                t = outer_product(blocks[r], unpack(grams[j - clus * count]))
                sums[i - clus * count] += pack(t)

        loop(blocks.shape[0], one)

    terms(ppairs, pblocks, pwin, pnear, parents)
    terms(cpairs, cblocks, win, near, boxes)


def remote(src, dst, sems, index, device):
    send, recv = sems
    return pltpu.make_async_remote_copy(
        src_ref=src, dst_ref=dst, send_sem=send.at[index], recv_sem=recv.at[index],
        device_id=device, device_id_type=MESH,
    )


def place():
    clus, n = lax.axis_index("clus"), lax.axis_size("clus")
    pair = lax.axis_index("pair")
    rows = lax.axis_size("pair") // CORES
    return clus, n, pair // CORES, rows, pair % CORES


def at_pair(clus, y, k):
    return (clus, y * CORES + k)


def meet(clus, n, y, rows, k, along):
    barrier = pltpu.get_barrier_semaphore()

    def tell(device):
        pl.semaphore_signal(barrier, inc=1, device_id=device, device_id_type=MESH)

    tell(at_pair(clus, y, 1 - k))
    for d in range(1, rows):
        tell(at_pair(clus, (y + d) % rows, k))
    peers = rows
    if along:
        for o in range(1, REACH + 1):
            for ok, other in ((clus >= o, clus - o), (clus + o < n, clus + o)):
                @pl.when(ok)
                def _():
                    tell(at_pair(other, y, k))
                peers = peers + ok.astype(jnp.int32)
    pl.semaphore_wait(barrier, peers)


def exchange_kernel(
    boxes, parents,
    basis_p, pbasis_p, far, pfar,
    win, pwin, own, pown,
    half_in, phalf_in, half, phalf, row_in, mine, up_in, pup_in,
    down_s, down_r, fwd_s, fwd_r, core_s, core_r, pcore_s, pcore_r,
    row_s, row_r, up_s, up_r, pup_s, pup_r, local_sem,
):
    clus, n, y, rows, k = place()
    hb, ph = boxes // CORES, parents // CORES
    qb = hb // rows
    meet(clus, n, y, rows, k, True)
    partner = at_pair(clus, y, 1 - k)
    reach = range(1, REACH + 1)
    order = (3, 1, 2, 0)
    odd = clus % 2 == 1
    even = clus % 2 == 0
    keep, give = pl.ds(k * hb, hb), pl.ds((1 - k) * hb, hb)
    pkeep, pgive = pl.ds(k * ph, ph), pl.ds((1 - k) * ph, ph)
    local = pltpu.make_async_copy(basis_p, win.at[0], local_sem.at[0])
    plocal = pltpu.make_async_copy(pbasis_p, pwin.at[0], local_sem.at[1])
    local.start()
    plocal.start()

    chunks = range(hb + 1)

    def held(o, i):
        return pwin.at[o, pkeep] if i == 0 else win.at[o, pl.ds(k * hb + i - 1, 1)]

    def first(i):
        return pbasis_p.at[pkeep] if i == 0 else basis_p.at[pl.ds(k * hb + i - 1, 1)]

    def down(src, o, i, to):
        return remote(src, held(o, i), (down_s, down_r), o * (hb + 1) + i, at_pair(to, y, k))

    def to_two(i):
        return down(first(i), 2, i, clus - 2)

    def to_one(i):
        return down(first(i), 1, i, clus - 1)

    def side(i):
        return down(held(2, i), 1, i, clus + 1)

    def to_three(i):
        return down(held(1, i), 3, i, clus - 2)

    def forward(o, i):
        return remote(held(o, i), held(o, i), (fwd_s, fwd_r), o * (hb + 1) + i, partner)

    core = [remote(far.at[o, give], half_in.at[o], (core_s, core_r), o, partner)
            for o in range(REACH + 1)]
    pcore = [remote(pfar.at[o, pgive], phalf_in.at[o], (pcore_s, pcore_r), o, partner)
             for o in range(REACH + 1)]
    for i in chunks:
        @pl.when(clus >= 2)
        def _():
            to_two(i).start()

        @pl.when(odd)
        def _():
            to_one(i).start()
    for o in order:
        core[o].start()
    for o in order:
        pcore[o].start()

    def pass_on(i):
        @pl.when(clus + 2 < n)
        def _():
            to_two(i).wait_recv()

            @pl.when(even)
            def _():
                side(i).start()

            forward(2, i).start()

        @pl.when(clus + 1 < n)
        def _():
            to_one(i).wait_recv()

            @pl.when(clus >= 2)
            def _():
                to_three(i).start()

            forward(1, i).start()

    row = {}
    for o in order:
        core[o].wait_recv()
        half[o] = far[o, keep] + half_in[o]
        for d in range(1, rows):
            to = (y + d) % rows
            row[o, d] = remote(
                half.at[o, pl.ds(to * qb, qb)], row_in.at[o, d - 1], (row_s, row_r),
                o * (rows - 1) + d - 1, at_pair(clus, to, k),
            )
            row[o, d].start()
    pup = {}
    for o in order:
        pcore[o].wait_recv()
        phalf[o] = pfar[o, pkeep] + phalf_in[o]
        if o:
            pup[o] = remote(phalf.at[o], pup_in.at[o - 1], (pup_s, pup_r), o, at_pair(clus + o, y, k))

            @pl.when(clus + o < n)
            def _():
                pup[o].start()

    def up(o, slot, to):
        return remote(mine.at[o], up_in.at[slot], (up_s, up_r), slot, at_pair(to, y, k))

    def gathered(o):
        total = half[o, pl.ds(y * qb, qb)]
        for d in range(1, rows):
            row[o, d].wait_recv()
            total = total + row_in[o, d - 1]
        mine[o] = total

    def rise(o):
        gathered(o)
        if o == 3:
            @pl.when(clus + 3 < n)
            def _():
                up(3, 3, clus + 2).start()
        if o == 1:
            @pl.when((clus >= 2) & (clus + 1 < n))
            def _():
                up(3, 3, clus + 2).wait_recv()
                mine[1] += up_in[3]

            @pl.when(even & (clus + 1 < n))
            def _():
                up(1, 1, clus + 1).start()

            @pl.when(odd & (clus + 1 < n))
            def _():
                up(1, 0, clus - 1).start()
        if o == 2:
            @pl.when(even & (clus + 2 < n))
            def _():
                up(1, 0, clus - 1).wait_recv()
                mine[2] += up_in[0]

            @pl.when(clus + 2 < n)
            def _():
                up(2, 2, clus + 2).start()

    pass_on(0)
    todo = list(order)
    for i in chunks[1:]:
        pass_on(i)
        if todo:
            rise(todo.pop(0))
    for o in todo:
        rise(o)
    for i in chunks:
        @pl.when(clus + 3 < n)
        def _():
            to_three(i).wait_recv()
            forward(3, i).start()

    own[...] = mine[0]
    pown[...] = phalf[0]
    for o in reach:
        @pl.when(clus >= o)
        def _():
            pup[o].wait_recv()
            pown[...] += pup_in[o - 1]

    @pl.when(odd)
    def _():
        up(1, 1, clus + 1).wait_recv()
        own[...] += up_in[1]

    @pl.when(clus >= 2)
    def _():
        up(2, 2, clus + 2).wait_recv()
        own[...] += up_in[2]

    local.wait()
    plocal.wait()
    for i in chunks:
        @pl.when(clus >= 2)
        def _():
            to_two(i).wait_send()

            @pl.when(clus + 1 < n)
            def _():
                to_three(i).wait_send()

        @pl.when(odd)
        def _():
            to_one(i).wait_send()

        @pl.when(even & (clus + 2 < n))
        def _():
            side(i).wait_send()

        for o in reach:
            @pl.when(clus + o < n)
            def _():
                forward(o, i).wait()
    for o in reach:
        @pl.when(clus + o < n)
        def _():
            pup[o].wait_send()

    @pl.when(clus + 3 < n)
    def _():
        up(3, 3, clus + 2).wait_send()

    @pl.when(clus + 2 < n)
    def _():
        up(2, 2, clus + 2).wait_send()

    @pl.when(even & (clus + 1 < n))
    def _():
        up(1, 1, clus + 1).wait_send()

    @pl.when(odd & (clus + 1 < n))
    def _():
        up(1, 0, clus - 1).wait_send()

    for o in range(REACH + 1):
        core[o].wait_send()
        pcore[o].wait_send()
        for d in range(1, rows):
            row[o, d].wait_send()


def finish_kernel(
    boxes, parents,
    near, pnear, own, pown, transfer, child_parent,
    out,
    half_in, phalf_in, weight, pwork, total, row_in,
    core_s, core_r, pcore_s, pcore_r, pw_s, pw_r, row_s, row_r, gat_s, gat_r, fwd_s, fwd_r,
):
    clus, n, y, rows, k = place()
    hb, ph = boxes // CORES, parents // CORES
    qb = hb // rows
    meet(clus, n, y, rows, k, False)
    partner = at_pair(clus, y, 1 - k)
    pkeep, pgive = pl.ds(k * ph, ph), pl.ds((1 - k) * ph, ph)
    pcore = remote(pnear.at[pgive], phalf_in, (pcore_s, pcore_r), 0, partner)
    core = remote(near.at[pl.ds((1 - k) * hb, hb)], half_in, (core_s, core_r), 0, partner)
    pcore.start()
    core.start()
    pcore.wait_recv()
    pwork[...] = pnear[pkeep] + phalf_in[...] + pown[...]
    weight[pkeep] = pwork[...]
    pw = remote(pwork, weight.at[pkeep], (pw_s, pw_r), 0, partner)
    pw.start()
    core.wait_recv()
    total[...] = near[pl.ds(k * hb, hb)] + half_in[...]
    pw.wait_recv()

    def lower(b):
        c = k * hb + b
        w = unpack(weight[child_parent[0, c]])
        total[b] += pack(outer_product(transfer[c], w))

    row = []
    for d in list(range(1, rows)) + [0]:
        to = (y + d) % rows
        loop(qb, lambda q: lower(to * qb + q))
        if d:
            copy = remote(
                total.at[pl.ds(to * qb, qb)], row_in.at[d - 1], (row_s, row_r), d - 1,
                at_pair(clus, to, k),
            )
            copy.start()
            row.append(copy)
    result = total[pl.ds(y * qb, qb)] + own[...]
    for d in range(1, rows):
        row[d - 1].wait_recv()
        result = result + row_in[d - 1]
    here = pl.ds(k * hb + y * qb, qb)
    out[here] = result
    gather = [
        remote(out.at[here], out.at[here], (gat_s, gat_r), d - 1, at_pair(clus, (y + d) % rows, k))
        for d in range(1, rows)
    ]
    for copy in gather:
        copy.start()
    forward = []
    for d in range(rows):
        there = here
        if d:
            gather[d - 1].wait_recv()
            there = pl.ds(k * hb + (y + rows - d) % rows * qb, qb)
        copy = remote(out.at[there], out.at[there], (fwd_s, fwd_r), d, partner)
        copy.start()
        forward.append(copy)
    for copy in forward:
        copy.wait()
    for copy in gather + row + [core, pcore, pw]:
        copy.wait_send()


def unpack_kernel(packed, out):
    out[0] = unpack(packed[0])


def per_device(
    child_basis, transfer, child_parent, upper_weight, child_pairs, child_blocks,
    parent_pairs, parent_blocks,
):
    boxes, extent = child_basis.shape[0], child_basis.shape[-1]
    parents = upper_weight.shape[0]
    rows = lax.axis_size("pair") // CORES
    hb, ph = boxes // CORES, parents // CORES
    qb = hb // rows
    spans = REACH + 1
    tall = extent * 3 // 4
    shape = lambda *lead: jax.ShapeDtypeStruct(lead + (tall, extent), F32)
    room = lambda *lead: pltpu.VMEM(lead + (tall, extent), F32)
    sems = lambda *counts: [pltpu.SemaphoreType.DMA((c,)) for c in counts for _ in range(2)]

    pbasis, basis_p, pbasis_p, far, pfar = pl.pallas_call(
        functools.partial(far_kernel, boxes, parents),
        out_shape=(
            jax.ShapeDtypeStruct(upper_weight.shape, F32),
            shape(boxes), shape(parents), shape(spans * boxes), shape(spans * parents),
        ),
        in_specs=[VMEM, VMEM, SMEM, SMEM, VMEM, SMEM, VMEM],
        out_specs=(VMEM,) * 5,
        name="far_terms",
    )(child_basis, transfer, child_parent, child_pairs, child_blocks, parent_pairs, parent_blocks)

    win, pwin, own, pown = pl.pallas_call(
        functools.partial(exchange_kernel, boxes, parents),
        out_shape=(shape(spans, boxes), shape(spans, parents), shape(qb), shape(ph)),
        in_specs=[VMEM] * 4,
        out_specs=(VMEM,) * 4,
        scratch_shapes=[
            room(spans, hb), room(spans, ph), room(spans, hb), room(spans, ph),
            room(spans, max(rows - 1, 1), qb), room(spans, qb), room(spans, qb), room(REACH, ph),
        ]
        + sems(
            spans * (hb + 1), spans * (hb + 1), spans, spans, spans * max(rows - 1, 1), spans, spans
        )
        + [pltpu.SemaphoreType.DMA((2,))],
        compiler_params=pltpu.CompilerParams(collective_id=0, has_side_effects=True),
        name="exchange",
    )(
        basis_p, pbasis_p,
        far.reshape(spans, boxes, tall, extent), pfar.reshape(spans, parents, tall, extent),
    )

    near, pnear = pl.pallas_call(
        functools.partial(near_kernel, boxes, parents, 1.0 / (rows * CORES)),
        out_shape=(shape(boxes), shape(parents)),
        in_specs=[SMEM, VMEM, VMEM, SMEM, VMEM, VMEM, VMEM],
        out_specs=(VMEM,) * 2,
        name="near_terms",
    )(
        child_pairs, child_blocks, win.reshape(spans * boxes, tall, extent),
        parent_pairs, parent_blocks, pwin.reshape(spans * parents, tall, extent), upper_weight,
    )

    packed = pl.pallas_call(
        functools.partial(finish_kernel, boxes, parents),
        out_shape=shape(boxes),
        in_specs=[VMEM] * 5 + [SMEM],
        out_specs=VMEM,
        scratch_shapes=[
            room(hb), room(ph), room(parents), room(ph), room(hb), room(max(rows - 1, 1), qb),
        ]
        + sems(1, 1, 1, max(rows - 1, 1), max(rows - 1, 1), rows),
        compiler_params=pltpu.CompilerParams(collective_id=1, has_side_effects=True),
        name="finish",
    )(near, pnear, own, pown, transfer, child_parent)

    child_weight = pl.pallas_call(
        unpack_kernel,
        grid=(boxes,),
        out_shape=jax.ShapeDtypeStruct(child_basis.shape, F32),
        in_specs=[pl.BlockSpec((1, tall, extent), lambda b: (b, 0, 0))],
        out_specs=pl.BlockSpec((1, extent, extent), lambda b: (b, 0, 0)),
        name="unfold",
    )(packed)
    return (child_weight, pbasis)


def solution(mesh):
    return jax.shard_map(
        per_device,
        mesh=mesh,
        in_specs=(
            P("clus", None, None),
            P("clus", None, None),
            P("clus", None),
            P("clus", None, None),
            P(("clus", "pair"), None),
            P(("clus", "pair"), None, None),
            P(("clus", "pair"), None),
            P(("clus", "pair"), None, None),
        ),
        out_specs=(P("clus", None, None), P("clus", None, None)),
        check_vma=False,
    )
```

```python
import functools

import jax
import jax.numpy as jnp
from jax import lax
from jax.experimental import pallas as pl
from jax.experimental.pallas import tpu as pltpu
from jax.sharding import PartitionSpec as P

REACH = 3
CORES = 2
MESH = pl.DeviceIdType.MESH
F32 = jnp.float32
VMEM = pl.BlockSpec(memory_space=pltpu.VMEM)
SMEM = pl.BlockSpec(memory_space=pltpu.SMEM)


def split(x):
    hi = x.astype(jnp.bfloat16)
    return hi, (x - hi.astype(F32)).astype(jnp.bfloat16)


def product(a, b, dims):
    (ah, al), (bh, bl) = a, b
    dot = functools.partial(
        lax.dot_general, dimension_numbers=(dims, ((), ())), preferred_element_type=F32
    )
    return dot(ah, bh) + (dot(ah, bl) + dot(al, bh))


NN = ((1,), (0,))
NT = ((1,), (1,))
TN = ((0,), (0,))


def pack(x):
    h, q = x.shape[0] // 2, x.shape[0] // 4
    low = jnp.concatenate([x[h : h + q, h:], x[h + q :, h:]], axis=1)
    return jnp.concatenate([x[:h], low], axis=0)


def unpack(p):
    n = p.shape[1]
    h, q = n // 2, n // 4
    top = p[:h]
    corner = jnp.concatenate([p[h:, :h], p[h:, h:]], axis=0)
    low = jnp.concatenate([top[:, h:].T, corner], axis=1)
    return jnp.concatenate([top, low], axis=0)


def loop(count, body):
    lax.fori_loop(0, count, lambda i, c: (body(i), c)[1], 0)


def outer_product(s, g):
    s, g = split(s), split(g)
    return product(split(product(s, g, NN)), s, NT)


def inner_product(s, g):
    s, g = split(s), split(g)
    return product(s, split(product(g, s, NN)), TN)


def spread(terms, slots, sums, count, weights):
    tall = terms.shape[1]
    step = tall // 6

    def two(t):
        picks = [
            [((slots(r) == 2 * t + e) & weights(r)).astype(F32) for r in range(terms.shape[0])]
            for e in range(2)
        ]

        def part(i):
            at = pl.ds(pl.multiple_of(i * step, step), step)
            totals = [None, None]
            for r in range(terms.shape[0]):
                value = terms[r, at, :]
                for e in range(2):
                    add = value * picks[e][r]
                    totals[e] = add if totals[e] is None else totals[e] + add
            for e in range(2):
                sums[2 * t + e, at, :] = totals[e]

        loop(6, part)

    loop(count // 2, two)


def remote(src, dst, sems, index, device):
    send, recv = sems
    return pltpu.make_async_remote_copy(
        src_ref=src, dst_ref=dst, send_sem=send.at[index], recv_sem=recv.at[index],
        device_id=device, device_id_type=MESH,
    )


def place():
    clus, n = lax.axis_index("clus"), lax.axis_size("clus")
    pair = lax.axis_index("pair")
    rows = lax.axis_size("pair") // CORES
    return clus, n, pair // CORES, rows, pair % CORES


def at_pair(clus, y, k):
    return (clus, y * CORES + k)


def meet(clus, n, y, rows, k, along):
    barrier = pltpu.get_barrier_semaphore()

    def tell(device):
        pl.semaphore_signal(barrier, inc=1, device_id=device, device_id_type=MESH)

    tell(at_pair(clus, y, 1 - k))
    for d in range(1, rows):
        tell(at_pair(clus, (y + d) % rows, k))
    peers = rows
    if along:
        for o in range(1, REACH + 1):
            for ok, other in ((clus >= o, clus - o), (clus + o < n, clus + o)):
                @pl.when(ok)
                def _():
                    tell(at_pair(other, y, k))
                peers = peers + ok.astype(jnp.int32)
    pl.semaphore_wait(barrier, peers)


def exchange_kernel(
    boxes, parents, scale,
    basis, transfer, child_parent, cpairs, cblocks, ppairs, pblocks, upper,
    pbasis, near, pnear, own, pown,
    win, pwin, terms, pterms, far, pfar,
    half_in, phalf_in, half, phalf, row_in, mine, up_in, pup_in,
    down_s, down_r, fwd_s, fwd_r, core_s, core_r, pcore_s, pcore_r,
    row_s, row_r, up_s, up_r, pup_s, pup_r,
):
    clus, n, y, rows, k = place()
    hb, ph = boxes // CORES, parents // CORES
    qb = hb // rows
    loop(boxes, lambda c: win.__setitem__(c, pack(basis[c])))
    meet(clus, n, y, rows, k, True)
    partner = at_pair(clus, y, 1 - k)
    reach = range(1, REACH + 1)
    order = (3, 1, 2, 0)
    odd = clus % 2 == 1
    even = clus % 2 == 0
    pkeep = pl.ds(k * ph, ph)

    chunks = range(hb + 1)

    def held(o, i):
        if i == hb:
            return pwin.at[pl.ds(o * parents + k * ph, ph)]
        return win.at[pl.ds(o * boxes + k * hb + i, 1)]

    def first(i):
        return held(0, i)

    def down(src, o, i, to):
        return remote(src, held(o, i), (down_s, down_r), o * (hb + 1) + i, at_pair(to, y, k))

    def to_two(i):
        return down(first(i), 2, i, clus - 2)

    def to_one(i):
        return down(first(i), 1, i, clus - 1)

    def side(i):
        return down(held(2, i), 1, i, clus + 1)

    def to_three(i):
        return down(held(1, i), 3, i, clus - 2)

    def forward(o, i):
        return remote(held(o, i), held(o, i), (fwd_s, fwd_r), o * (hb + 1) + i, partner)

    core = [remote(far.at[pl.ds(o * boxes + (1 - k) * hb, hb)], half_in.at[o], (core_s, core_r), o, partner)
            for o in range(REACH + 1)]
    pcore = [remote(pfar.at[pl.ds(o * parents + (1 - k) * ph, ph)], phalf_in.at[o], (pcore_s, pcore_r), o, partner)
             for o in range(REACH + 1)]

    def launch(i):
        @pl.when(clus >= 2)
        def _():
            to_two(i).start()

        @pl.when(odd)
        def _():
            to_one(i).start()

    def pass_on(i):
        @pl.when(clus + 2 < n)
        def _():
            to_two(i).wait_recv()

            @pl.when(even)
            def _():
                side(i).start()

            forward(2, i).start()

        @pl.when(clus + 1 < n)
        def _():
            to_one(i).wait_recv()

            @pl.when(clus >= 2)
            def _():
                to_three(i).start()

            forward(1, i).start()

    def usable(pairs):
        return lambda r: pairs[r, 0] >= 0

    def slot(pairs, side, count):
        return lambda r: pairs[r, side] - clus * count

    def inner(pairs, blocks, grams, count, out, start, stop):
        def one(t):
            r = start + t
            i = jnp.clip(pairs[r, 0] - clus * count, 0, count - 1)
            out[r] = pack(inner_product(blocks[r], grams[i]))

        loop(stop - start, one)

    def outer(pairs, blocks, grams, count, out):
        def one(r):
            j = jnp.clip(pairs[r, 1] - clus * count, 0, grams.shape[0] - 1)
            j = jnp.where(pairs[r, 0] >= 0, j, 0)
            out[r] = pack(outer_product(blocks[r], unpack(grams[j])))

        loop(blocks.shape[0], one)

    slots = cblocks.shape[0]
    for i in range(hb):
        launch(i)
    pbasis[...] = jnp.zeros_like(pbasis)

    def lift(c):
        t = inner_product(transfer[c], basis[c])
        for p in range(parents):
            pbasis[p] += t * (child_parent[0, c] == p).astype(F32)

    loop(boxes, lift)
    for p in range(parents):
        pwin[p] = pack(pbasis[p])
    launch(hb)
    inner(cpairs, cblocks, basis, boxes, terms, 0, slots // 2)
    pass_on(0)
    pass_on(1)
    inner(cpairs, cblocks, basis, boxes, terms, slots // 2, slots)
    spread(terms, slot(cpairs, 1, boxes), far, (REACH + 1) * boxes, usable(cpairs))
    for o in order:
        core[o].start()
    pass_on(2)
    inner(ppairs, pblocks, pbasis, parents, pterms, 0, pblocks.shape[0])
    spread(pterms, slot(ppairs, 1, parents), pfar, (REACH + 1) * parents, usable(ppairs))
    for o in order:
        pcore[o].start()
    row = {}
    for o in order:
        core[o].wait_recv()
        half[o] = far[pl.ds(o * boxes + k * hb, hb)] + half_in[o]
        for d in range(1, rows):
            to = (y + d) % rows
            row[o, d] = remote(
                half.at[o, pl.ds(to * qb, qb)], row_in.at[o, d - 1], (row_s, row_r),
                o * (rows - 1) + d - 1, at_pair(clus, to, k),
            )
            row[o, d].start()
    pup = {}
    for o in order:
        pcore[o].wait_recv()
        phalf[o] = pfar[pl.ds(o * parents + k * ph, ph)] + phalf_in[o]
        if o:
            pup[o] = remote(phalf.at[o], pup_in.at[o - 1], (pup_s, pup_r), o, at_pair(clus + o, y, k))

            @pl.when(clus + o < n)
            def _():
                pup[o].start()

    def up(o, slot, to):
        return remote(mine.at[o], up_in.at[slot], (up_s, up_r), slot, at_pair(to, y, k))

    def gathered(o):
        total = half[o, pl.ds(y * qb, qb)]
        for d in range(1, rows):
            row[o, d].wait_recv()
            total = total + row_in[o, d - 1]
        mine[o] = total

    def rise(o):
        gathered(o)
        if o == 3:
            @pl.when(clus + 3 < n)
            def _():
                up(3, 3, clus + 2).start()
        if o == 1:
            @pl.when((clus >= 2) & (clus + 1 < n))
            def _():
                up(3, 3, clus + 2).wait_recv()
                mine[1] += up_in[3]

            @pl.when(even & (clus + 1 < n))
            def _():
                up(1, 1, clus + 1).start()

            @pl.when(odd & (clus + 1 < n))
            def _():
                up(1, 0, clus - 1).start()
        if o == 2:
            @pl.when(even & (clus + 2 < n))
            def _():
                up(1, 0, clus - 1).wait_recv()
                mine[2] += up_in[0]

            @pl.when(clus + 2 < n)
            def _():
                up(2, 2, clus + 2).start()

    pass_on(hb)
    for i in range(3, hb):
        pass_on(i)
    rise(3)

    def settle(i):
        @pl.when(clus + 3 < n)
        def _():
            to_three(i).wait_recv()
            forward(3, i).start()

    settle(hb)
    rise(1)
    for i in range(hb):
        settle(i)
    for i in chunks:
        for o in reach:
            @pl.when(clus + o < n)
            def _():
                forward(o, i).wait_recv()
    outer(ppairs, pblocks, pwin, parents, pterms)
    spread(pterms, slot(ppairs, 0, parents), pnear, parents, usable(ppairs))
    for p in range(parents):
        pnear[p] += pack(upper[p]) * scale
    rise(2)
    outer(cpairs, cblocks, win, boxes, terms)
    spread(terms, slot(cpairs, 0, boxes), near, boxes, usable(cpairs))
    rise(0)
    own[...] = mine[0]
    pown[...] = phalf[0]
    for o in reach:
        @pl.when(clus >= o)
        def _():
            pup[o].wait_recv()
            pown[...] += pup_in[o - 1]

    @pl.when(odd)
    def _():
        up(1, 1, clus + 1).wait_recv()
        own[...] += up_in[1]

    @pl.when(clus >= 2)
    def _():
        up(2, 2, clus + 2).wait_recv()
        own[...] += up_in[2]

    for i in chunks:
        @pl.when(clus >= 2)
        def _():
            to_two(i).wait_send()

            @pl.when(clus + 1 < n)
            def _():
                to_three(i).wait_send()

        @pl.when(odd)
        def _():
            to_one(i).wait_send()

        @pl.when(even & (clus + 2 < n))
        def _():
            side(i).wait_send()

        for o in reach:
            @pl.when(clus + o < n)
            def _():
                forward(o, i).wait_send()
    for o in reach:
        @pl.when(clus + o < n)
        def _():
            pup[o].wait_send()

    @pl.when(clus + 3 < n)
    def _():
        up(3, 3, clus + 2).wait_send()

    @pl.when(clus + 2 < n)
    def _():
        up(2, 2, clus + 2).wait_send()

    @pl.when(even & (clus + 1 < n))
    def _():
        up(1, 1, clus + 1).wait_send()

    @pl.when(odd & (clus + 1 < n))
    def _():
        up(1, 0, clus - 1).wait_send()

    for o in range(REACH + 1):
        core[o].wait_send()
        pcore[o].wait_send()
        for d in range(1, rows):
            row[o, d].wait_send()


def finish_kernel(
    boxes, parents,
    near, pnear, own, pown, transfer, child_parent,
    out,
    half_in, phalf_in, weight, pwork, total, row_in,
    core_s, core_r, pcore_s, pcore_r, pw_s, pw_r, row_s, row_r, gat_s, gat_r, fwd_s, fwd_r,
):
    clus, n, y, rows, k = place()
    hb, ph = boxes // CORES, parents // CORES
    qb = hb // rows
    meet(clus, n, y, rows, k, False)
    partner = at_pair(clus, y, 1 - k)
    pkeep, pgive = pl.ds(k * ph, ph), pl.ds((1 - k) * ph, ph)
    pcore = remote(pnear.at[pgive], phalf_in, (pcore_s, pcore_r), 0, partner)
    core = remote(near.at[pl.ds((1 - k) * hb, hb)], half_in, (core_s, core_r), 0, partner)
    pcore.start()
    core.start()
    pcore.wait_recv()
    pwork[...] = pnear[pkeep] + phalf_in[...] + pown[...]
    weight[pkeep] = pwork[...]
    pw = remote(pwork, weight.at[pkeep], (pw_s, pw_r), 0, partner)
    pw.start()
    core.wait_recv()
    total[...] = near[pl.ds(k * hb, hb)] + half_in[...]
    pw.wait_recv()

    def lower(b):
        c = k * hb + b
        w = unpack(weight[child_parent[0, c]])
        total[b] += pack(outer_product(transfer[c], w))

    row = []
    for d in list(range(1, rows)) + [0]:
        to = (y + d) % rows
        loop(qb, lambda q: lower(to * qb + q))
        if d:
            copy = remote(
                total.at[pl.ds(to * qb, qb)], row_in.at[d - 1], (row_s, row_r), d - 1,
                at_pair(clus, to, k),
            )
            copy.start()
            row.append(copy)
    result = total[pl.ds(y * qb, qb)] + own[...]
    for d in range(1, rows):
        row[d - 1].wait_recv()
        result = result + row_in[d - 1]
    here = pl.ds(k * hb + y * qb, qb)
    out[here] = result
    gather = [
        remote(out.at[here], out.at[here], (gat_s, gat_r), d - 1, at_pair(clus, (y + d) % rows, k))
        for d in range(1, rows)
    ]
    for copy in gather:
        copy.start()
    forward = []
    for d in range(rows):
        there = here
        if d:
            gather[d - 1].wait_recv()
            there = pl.ds(k * hb + (y + rows - d) % rows * qb, qb)
        copy = remote(out.at[there], out.at[there], (fwd_s, fwd_r), d, partner)
        copy.start()
        forward.append(copy)
    for copy in forward:
        copy.wait()
    for copy in gather + row + [core, pcore, pw]:
        copy.wait_send()


def unpack_kernel(packed, out):
    out[0] = unpack(packed[0])


def per_device(
    child_basis, transfer, child_parent, upper_weight, child_pairs, child_blocks,
    parent_pairs, parent_blocks,
):
    boxes, extent = child_basis.shape[0], child_basis.shape[-1]
    parents = upper_weight.shape[0]
    rows = lax.axis_size("pair") // CORES
    hb, ph = boxes // CORES, parents // CORES
    qb = hb // rows
    spans = REACH + 1
    tall = extent * 3 // 4
    shape = lambda *lead: jax.ShapeDtypeStruct(lead + (tall, extent), F32)
    room = lambda *lead: pltpu.VMEM(lead + (tall, extent), F32)
    sems = lambda *counts: [pltpu.SemaphoreType.DMA((c,)) for c in counts for _ in range(2)]

    cslots, pslots = child_blocks.shape[0], parent_blocks.shape[0]
    pbasis, near, pnear, own, pown = pl.pallas_call(
        functools.partial(exchange_kernel, boxes, parents, 1.0 / (rows * CORES)),
        out_shape=(
            jax.ShapeDtypeStruct(upper_weight.shape, F32),
            shape(boxes), shape(parents), shape(qb), shape(ph),
        ),
        in_specs=[VMEM, VMEM, SMEM, SMEM, VMEM, SMEM, VMEM, VMEM],
        out_specs=(VMEM,) * 5,
        scratch_shapes=[
            room(spans * boxes), room(spans * parents), room(cslots), room(pslots),
            room(spans * boxes), room(spans * parents),
            room(spans, hb), room(spans, ph), room(spans, hb), room(spans, ph),
            room(spans, max(rows - 1, 1), qb), room(spans, qb), room(spans, qb), room(REACH, ph),
        ]
        + sems(
            spans * (hb + 1), spans * (hb + 1), spans, spans, spans * max(rows - 1, 1), spans, spans
        ),
        compiler_params=pltpu.CompilerParams(collective_id=0, has_side_effects=True),
        name="exchange",
    )(
        child_basis, transfer, child_parent, child_pairs, child_blocks, parent_pairs,
        parent_blocks, upper_weight,
    )

    packed = pl.pallas_call(
        functools.partial(finish_kernel, boxes, parents),
        out_shape=shape(boxes),
        in_specs=[VMEM] * 5 + [SMEM],
        out_specs=VMEM,
        scratch_shapes=[
            room(hb), room(ph), room(parents), room(ph), room(hb), room(max(rows - 1, 1), qb),
        ]
        + sems(1, 1, 1, max(rows - 1, 1), max(rows - 1, 1), rows),
        compiler_params=pltpu.CompilerParams(collective_id=1, has_side_effects=True),
        name="finish",
    )(near, pnear, own, pown, transfer, child_parent)

    child_weight = pl.pallas_call(
        unpack_kernel,
        grid=(boxes,),
        out_shape=jax.ShapeDtypeStruct(child_basis.shape, F32),
        in_specs=[pl.BlockSpec((1, tall, extent), lambda b: (b, 0, 0))],
        out_specs=pl.BlockSpec((1, extent, extent), lambda b: (b, 0, 0)),
        name="unfold",
    )(packed)
    return (child_weight, pbasis)


def solution(mesh):
    return jax.shard_map(
        per_device,
        mesh=mesh,
        in_specs=(
            P("clus", None, None),
            P("clus", None, None),
            P("clus", None),
            P("clus", None, None),
            P(("clus", "pair"), None),
            P(("clus", "pair"), None, None),
            P(("clus", "pair"), None),
            P(("clus", "pair"), None, None),
        ),
        out_specs=(P("clus", None, None), P("clus", None, None)),
        check_vma=False,
    )
```
